32 devices in a mesh: rep: 8 (over z, core), shard: 4 (over y, x).
Axes of the slice: x: 2, y: 2, z: 4, core: 2. Of those that a mesh axis runs over, the one named last changes fastest.
Arguments:
- tokens: bfloat16 [16384, 768], P(('rep', 'shard')), may hold values from -6 to 6
- cotangent: bfloat16 [16384, 768], P(('rep', 'shard')), may hold values from -6 to 6
- segment_ids: int32 [32, 512], P(('rep', 'shard')), may hold values from 0 to 5, never falling along the last dimension, each value on 1 to 256 neighbouring positions
- send_order: int32 [32, 512], P(('rep', 'shard')), may hold values from 0 to 511, each once within a row
- pack_order: int32 [32, 512], P(('rep', 'shard')), may hold values from 0 to 511, each once within a row
- query_weight: bfloat16 [768, 768], P('shard'), may hold values from -0.21875 to 0.21875
- key_weight: bfloat16 [768, 768], P('shard'), may hold values from -0.21875 to 0.21875
- value_weight: bfloat16 [768, 768], P('shard'), may hold values from -0.21875 to 0.21875
- out_weight: bfloat16 [768, 768], P('shard'), may hold values from -0.875 to 0.875
- up_weight: bfloat16 [768, 3072], P('shard'), may hold values from -0.21875 to 0.21875
- down_weight: bfloat16 [3072, 768], P('shard'), may hold values from -0.109375 to 0.109375
- query_bias: bfloat16 [768], P('shard'), may hold values from -3 to 3
- value_bias: bfloat16 [768], P('shard'), may hold values from -3 to 3
- out_bias: bfloat16 [768], P('shard'), may hold values from -3 to 3
- up_bias: bfloat16 [3072], P('shard'), may hold values from -3 to 3
- down_bias: bfloat16 [768], P('shard'), may hold values from -3 to 3
- first_gain: bfloat16 [768], P('shard'), may hold values from 0.5 to 1.5
- first_shift: bfloat16 [768], P('shard'), may hold values from -3 to 3
- second_gain: bfloat16 [768], P('shard'), may hold values from 0.5 to 1.5
- second_shift: bfloat16 [768], P('shard'), may hold values from -3 to 3
Outputs:
- layer_out: bfloat16 [16384, 768], P(('rep', 'shard'))
- grad_tokens: bfloat16 [16384, 768], P(('rep', 'shard'))
- grad_query_weight: float32 [768, 768], P('shard')
- grad_key_weight: float32 [768, 768], P('shard')
- grad_value_weight: float32 [768, 768], P('shard')
- grad_out_weight: float32 [768, 768], P('shard')
- grad_up_weight: float32 [768, 3072], P('shard')
- grad_down_weight: float32 [3072, 768], P('shard')
- grad_query_bias: float32 [768], P('shard')
- grad_value_bias: float32 [768], P('shard')
- grad_out_bias: float32 [768], P('shard')
- grad_up_bias: float32 [3072], P('shard')
- grad_down_bias: float32 [768], P('shard')
- grad_first_gain: float32 [768], P('shard')
- grad_first_shift: float32 [768], P('shard')
- grad_second_gain: float32 [768], P('shard')
- grad_second_shift: float32 [768], P('shard')
The draws below stay inside these ranges and needn't reach their ends.
Inputs may be any that keep to these rules, and one draw needn't show every extreme that they name: `segment_ids`: in each row of one device's packed rows the ids never fall; every id from 0 to 5 covers 1 to 256 consecutive rows, and one covers exactly 256. `send_order`: each row is a permutation of 0 to 511. `pack_order`: each row is a permutation of 0 to 511.
All inputs are finite; a program needn't handle non-finite values.
Results may differ from the reference program's by a relative error of at most 0.02.
Values may be sent and summed in bfloat16 or wider, within the bound.
No kernel may reach another device: no remote copies, remote signals or barrier semaphores. Data moves between devices by JAX's collectives and lax.ppermute only.
A program may use at most 128 MiB of HBM per device.

```python
import math
import jax
import jax.numpy as jnp
import numpy as np
from jax import lax

D = 768
FF = 3072
HEADS = 12
HEAD_DIM = 64
TOK_DEV = 512
SEQS_DEV = 6
TOKENS = 16384
DEVICES = 32


def levels(stream_key, shape, pieces, least, top_value):
    gain, own = 1.0, jax.random.fold_in(stream_key, 6)
    for axis_at, shards_of in pieces:
        draws = jnp.exp(jax.random.uniform(jax.random.fold_in(own, axis_at), (shards_of,), jnp.float32, least / len(pieces), top_value / len(pieces)))
        gain = gain * jnp.repeat(draws, shape[axis_at] // shards_of).reshape([-1 if axis == axis_at else 1 for axis in range(len(shape))])
    return gain


def split_up(amount, total, reach, slope):
    loads = [(1 << 20) // math.isqrt(standing ** slope) + 1 for standing in range(2, amount + 1)]
    surplus, counts = total - reach - (amount - 1), [1] * (amount - 1)
    while surplus > 0:
        free = [i for i in range(amount - 1) if counts[i] < reach]
        pool, left = sum([loads[i] for i in free]), surplus
        for i in free:
            addition = min(reach - counts[i], max(1, left * loads[i] // pool), surplus)
            counts[i] = counts[i] + addition
            surplus = surplus - addition
    return np.array([reach] + counts)


def uneven_parts(rng, number_of, total, reach, slope):
    if number_of == 2:
        one = jax.random.randint(rng, (), max(1, total - reach), min(reach, total - 1) + 1)
        return jnp.stack([one, total - one])
    lengths = jnp.asarray(split_up(number_of, total, reach, slope), jnp.int32)
    pairs = (number_of - 1) // 2
    donor, sink = lengths[1:1 + 2 * pairs:2], lengths[2:2 + 2 * pairs:2]
    margin = jnp.minimum(donor - 1, reach - sink)
    passed = jax.random.randint(jax.random.fold_in(rng, 1), (pairs,), 0, 1 << 20) % (margin + 1)
    lengths = lengths.at[1:1 + 2 * pairs:2].set(donor - passed).at[2:2 + 2 * pairs:2].set(sink + passed)
    return lengths[jax.random.permutation(jax.random.fold_in(rng, 2), number_of)]


def gaussian(stream_key, shape, deviation, limit, shards=(), kind=jnp.bfloat16):
    values = jax.random.normal(stream_key, shape, jnp.float32) * deviation
    if len(shards) > 0:
        values = levels(stream_key, shape, shards, -0.22, 0.18) * values
    return jnp.clip(values, min=-limit, max=limit).astype(kind)


def setup_inputs(seed: int = 0) -> dict:
    key_of = jax.random.split(jax.random.key(seed), 21)
    tokens = gaussian(key_of[0], (TOKENS, D), 1.0, 6.0, ((0, 32),))
    cotangent = gaussian(key_of[1], (TOKENS, D), 1.0, 6.0, ((0, 32),))
    segment_ids = jax.vmap(lambda own: jnp.searchsorted(jnp.cumsum(uneven_parts(own, SEQS_DEV, TOK_DEV, TOK_DEV // 2, 1)), jnp.arange(TOK_DEV), side="right"))(jax.random.split(key_of[2], DEVICES)).reshape((DEVICES, TOK_DEV)).astype(jnp.int32)
    send_order = jax.vmap(lambda own: jax.random.permutation(own, TOK_DEV))(jax.random.split(key_of[3], DEVICES)).reshape((DEVICES, TOK_DEV)).astype(jnp.int32)
    pack_order = jax.vmap(lambda own: jax.random.permutation(own, TOK_DEV))(jax.random.split(key_of[4], DEVICES)).reshape((DEVICES, TOK_DEV)).astype(jnp.int32)
    query_weight = gaussian(key_of[5], (D, D), D ** -0.5, 0.21875, ((0, 4),))
    key_weight = gaussian(key_of[6], (D, D), D ** -0.5, 0.21875, ((0, 4),))
    value_weight = gaussian(key_of[7], (D, D), D ** -0.5, 0.21875, ((0, 4),))
    out_weight = gaussian(key_of[8], (D, D), (D // 16) ** -0.5, 0.875, ((0, 4),))
    up_weight = gaussian(key_of[9], (D, FF), D ** -0.5, 0.21875, ((0, 4),))
    down_weight = gaussian(key_of[10], (FF, D), FF ** -0.5, 0.109375, ((0, 4),))
    query_bias = gaussian(key_of[11], (D,), 0.5, 3.0, ((0, 4),))
    value_bias = gaussian(key_of[12], (D,), 0.5, 3.0, ((0, 4),))
    out_bias = gaussian(key_of[13], (D,), 0.5, 3.0, ((0, 4),))
    up_bias = gaussian(key_of[14], (FF,), 0.5, 3.0, ((0, 4),))
    down_bias = gaussian(key_of[15], (D,), 0.5, 3.0, ((0, 4),))
    first_gain = jnp.clip(1.0 + 0.1 * jax.random.normal(key_of[16], (D,), jnp.float32), 0.5, 1.5).astype(jnp.bfloat16)
    first_shift = gaussian(key_of[17], (D,), 0.5, 3.0, ((0, 4),))
    second_gain = jnp.clip(1.0 + 0.1 * jax.random.normal(key_of[18], (D,), jnp.float32), 0.5, 1.5).astype(jnp.bfloat16)
    second_shift = gaussian(key_of[19], (D,), 0.5, 3.0, ((0, 4),))
    return dict(tokens=tokens, cotangent=cotangent, segment_ids=segment_ids, send_order=send_order, pack_order=pack_order, query_weight=query_weight, key_weight=key_weight, value_weight=value_weight, out_weight=out_weight, up_weight=up_weight, down_weight=down_weight, query_bias=query_bias, value_bias=value_bias, out_bias=out_bias, up_bias=up_bias, down_bias=down_bias, first_gain=first_gain, first_shift=first_shift, second_gain=second_gain, second_shift=second_shift)


@jax.custom_vjp
def low(v):
    return lax.optimization_barrier(v.astype(jnp.bfloat16)).astype(jnp.float32)

@jax.custom_vjp
def low_back(v):
    return v

def low_keep(v):
    return (low(v), None)

def low_pass(kept, grad):
    return (grad,)

def back_keep(v):
    return (v, None)

def back_low(kept, grad):
    return (low(grad),)
low.defvjp(low_keep, low_pass)
low_back.defvjp(back_keep, back_low)
epsilon = 1e-12
highest = lax.Precision.HIGHEST

def matmul(left_rows, right_rows):
    return jnp.dot(left_rows, right_rows, precision=highest)

def layer_norm(summed):
    center = summed - lax.optimization_barrier(jnp.mean(summed, -1, keepdims=True))
    return center * lax.rsqrt(lax.optimization_barrier(jnp.mean(center * center, -1, keepdims=True)) + epsilon)

def device_layer(params, inputs, segments):
    query_weight, key_weight, value_weight, out_weight, up_weight, down_weight, query_bias, value_bias, out_bias, up_bias, down_bias, first_gain, first_shift, second_gain, second_shift = params
    row_count = inputs.shape[0]
    head_shape = (row_count, HEADS, HEAD_DIM)
    queries = low_back(low(matmul(inputs, query_weight) + query_bias)).reshape(head_shape)
    key_rows = low_back(low(matmul(inputs, key_weight))).reshape(head_shape)
    value_rows = low_back(low(matmul(inputs, value_weight) + value_bias)).reshape(head_shape)
    logits = low_back(jnp.einsum('qhd,khd->hqk', queries, key_rows, precision=highest) * HEAD_DIM ** (-0.5))
    same_segment = segments[:, None] == segments[None, :]
    logits = jnp.where(same_segment[None], logits, -1e+30)
    row_max = lax.optimization_barrier(jnp.max(logits, -1, keepdims=True))
    exponent = jnp.exp(logits - row_max)
    softmax_rows = exponent / lax.optimization_barrier(jnp.sum(exponent, -1, keepdims=True))
    attended = jnp.einsum('hqk,khd->qhd', low(softmax_rows), value_rows, precision=highest)
    attended = low_back(low(attended.reshape(row_count, HEADS * HEAD_DIM)))
    branch = low_back(matmul(attended, out_weight) + out_bias)
    normed_one = low(layer_norm(inputs + branch) * first_gain + first_shift)
    pre_act = low_back(matmul(normed_one, up_weight) + up_bias)
    activated = low(jax.nn.gelu(pre_act, approximate=False))
    ffn_out = low_back(matmul(activated, down_weight) + down_bias)
    return layer_norm(normed_one + ffn_out) * second_gain + second_shift

def reference(tokens, cotangent, segment_ids, send_order, pack_order, query_weight, key_weight, value_weight, out_weight, up_weight, down_weight, query_bias, value_bias, out_bias, up_bias, down_bias, first_gain, first_shift, second_gain, second_shift):
    piece_rows = TOK_DEV // DEVICES

    def to_device(matrix):
        sectioned = jnp.take_along_axis(matrix.reshape(DEVICES, TOK_DEV, D), send_order[:, :, None], axis=1)
        arrived = sectioned.reshape(DEVICES, DEVICES, piece_rows, D).transpose(1, 0, 2, 3).reshape(DEVICES, TOK_DEV, D)
        return jnp.take_along_axis(arrived, pack_order[:, :, None], axis=1)

    def to_arrival(matrix):
        back_pack = jnp.argsort(pack_order, axis=1).astype(jnp.int32)
        back_send = jnp.argsort(send_order, axis=1).astype(jnp.int32)
        arrived = jnp.take_along_axis(matrix, back_pack[:, :, None], axis=1)
        sectioned = arrived.reshape(DEVICES, DEVICES, piece_rows, D).transpose(1, 0, 2, 3).reshape(DEVICES, TOK_DEV, D)
        return jnp.take_along_axis(sectioned, back_send[:, :, None], axis=1).reshape(TOKENS, D)
    params = tuple((weight.astype(jnp.float32) for weight in (query_weight, key_weight, value_weight, out_weight, up_weight, down_weight, query_bias, value_bias, out_bias, up_bias, down_bias, first_gain, first_shift, second_gain, second_shift)))
    inputs = to_device(tokens.astype(jnp.float32))
    grads_in = to_device(cotangent.astype(jnp.float32))

    def whole(weights_all, rows_in):

        def one_device(device_item):
            return device_layer(weights_all, device_item[0], device_item[1])
        return lax.map(jax.checkpoint(one_device), (rows_in, segment_ids))
    result, pullback = jax.vjp(whole, params, inputs)
    grad_params, grad_inputs = pullback(grads_in)
    g_query, g_key, g_value, g_out, g_up, g_down, g_query_bias, g_value_bias, g_out_bias, g_up_bias, g_down_bias, g_first_gain, g_first_shift, g_second_gain, g_second_shift = grad_params
    layer_out = to_arrival(result).astype(jnp.bfloat16)
    grad_tokens = to_arrival(grad_inputs).astype(jnp.bfloat16)
    return (layer_out, grad_tokens, g_query, g_key, g_value, g_out, g_up, g_down, g_query_bias, g_value_bias, g_out_bias, g_up_bias, g_down_bias, g_first_gain, g_first_shift, g_second_gain, g_second_shift)
```

```python
import functools

import jax
import jax.numpy as jnp
from jax import lax
from jax.experimental import pallas as pl
from jax.experimental.pallas import tpu as pltpu
from jax.sharding import PartitionSpec as P

HEADS = 12
HEAD_DIM = 64
VEC_ROWS = 32

epsilon = 1e-12
inv_root_two = 0.7071067811865476
inv_root_tau = 0.3989422804014327
BF = jnp.bfloat16
F32 = jnp.float32
ANY = pl.BlockSpec(memory_space=pl.ANY)
SMEM = pl.BlockSpec(memory_space=pltpu.SMEM)


def project(left_rows, weight):
    return jnp.dot(left_rows, weight, preferred_element_type=F32)


def project_back(left_rows, weight):
    return jnp.einsum("ti,ji->tj", left_rows, weight, preferred_element_type=F32)


def outer_sum(left_rows, right_rows):
    return jnp.einsum("ti,tj->ij", left_rows, right_rows, preferred_element_type=F32)


def normalize(summed):
    center = summed - jnp.mean(summed, -1, keepdims=True)
    spread = lax.rsqrt(jnp.mean(center * center, -1, keepdims=True) + epsilon)
    return (center * spread, spread)


def norm_back(gradient, normed, spread):
    return spread * (
        gradient
        - jnp.mean(gradient, -1, keepdims=True)
        - normed * jnp.mean(gradient * normed, -1, keepdims=True)
    )


def inverse(order_rows):
    return (
        jnp.zeros_like(order_rows)
        .at[order_rows]
        .set(jnp.arange(order_rows.shape[0], dtype=jnp.int32))
    )


class Comm:
    def __init__(self, mesh):
        self.S = mesh.shape["shard"]
        self.R = mesh.shape["rep"]
        self.Z = self.R // 2
        self.groups = [[r for r in range(self.R) if r % 2 == c] for c in range(2)]

    def across(self, x, mask):
        return lax.ppermute(x, "shard", [(i, i ^ mask) for i in range(self.S)])

    def partner(self, x):
        return lax.ppermute(x, "rep", [(i, i ^ 1) for i in range(self.R)])

    def over_z(self, x):
        return lax.all_to_all(
            x, "rep", split_axis=0, concat_axis=0, tiled=True, axis_index_groups=self.groups
        )

    def gather(self, part):
        if self.S != 4:
            got = [(r, 0, self.across(part, r)) for r in range(1, self.S)]
        else:
            half = part.shape[0] // 2
            from_x = self.across(part, 1)
            from_y = self.across(part, 2)
            low = self.across(from_x[:half], 2)
            high = self.across(from_y[half:], 1)
            got = [(1, 0, from_x), (2, 0, from_y), (3, 0, low), (3, half, high)]
        return got + [(r, at, self.partner(piece)) for r, at, piece in got]

    def reduce_shard(self, parts, s):
        rel = [lax.dynamic_index_in_dim(parts, s ^ r, 0, keepdims=False) for r in range(self.S)]
        if self.S != 4:
            total = rel[0].astype(F32)
            for r in range(1, self.S):
                total = total + self.across(rel[r], r).astype(F32)
            return total.astype(BF)
        half = parts.shape[1] // 2

        def add(a, b):
            return (a.astype(F32) + b.astype(F32)).astype(BF)

        low = self.across(jnp.concatenate([rel[1][:half], rel[3][:half]]), 1)
        high = self.across(jnp.concatenate([rel[2][half:], rel[3][half:]]), 2)
        low2 = self.across(add(rel[2][:half], low[half:]), 2)
        high1 = self.across(add(rel[1][half:], high[half:]), 1)
        low0 = rel[0][:half].astype(F32) + low[:half].astype(F32) + low2.astype(F32)
        high0 = rel[0][half:].astype(F32) + high[:half].astype(F32) + high1.astype(F32)
        return jnp.concatenate([low0, high0]).astype(BF)

    def reduce(self, mine, theirs, s):
        summed = (mine.astype(F32) + self.partner(theirs).astype(F32)).astype(BF)
        own = self.reduce_shard(summed, s)
        h, n = own.shape
        spread = self.over_z(own.reshape(self.Z, h // self.Z, n))
        total = jnp.sum(spread.astype(F32), 0).astype(BF)
        again = self.over_z(jnp.broadcast_to(total[None], (self.Z,) + total.shape))
        half = again.reshape(h, n)
        return half, self.partner(half)


def assemble(where, owns, got, shard_rows, halves):
    count = len(owns)
    S = where[2]

    def body(pos, *refs):
        own_refs = refs[:count]
        piece_refs = refs[count : count + len(got)]
        outs = refs[count + len(got) : 2 * count + len(got)]
        sem = refs[-1]
        s = pos[0]
        c = pos[1]
        copies = []
        for w in range(count):
            copies.append((own_refs[w], outs[w].at[pl.ds(s * shard_rows[w], shard_rows[w])]))
        for i, (r, at, piece) in enumerate(got):
            core = c if i < len(got) // 2 else 1 - c
            base = 0
            for w in range(count):
                lo, hi = max(at, base), min(at + piece.shape[0], base + halves[w])
                if lo < hi:
                    row = (s ^ r) * shard_rows[w] + core * halves[w] + (lo - base)
                    row = pl.multiple_of(row, 8)
                    copies.append(
                        (piece_refs[i].at[pl.ds(lo - at, hi - lo)], outs[w].at[pl.ds(row, hi - lo)])
                    )
                base += halves[w]
        copies = [pltpu.make_async_copy(a, b, sem.at[i]) for i, (a, b) in enumerate(copies)]
        for copy in copies:
            copy.start()
        for copy in copies:
            copy.wait()

    total = count + sum(
        sum(
            1
            for w in range(count)
            if max(at, sum(halves[:w])) < min(at + piece.shape[0], sum(halves[: w + 1]))
        )
        for r, at, piece in got
    )
    return pl.pallas_call(
        body,
        out_shape=[
            jax.ShapeDtypeStruct((S * rows, own.shape[1]), BF) for rows, own in zip(shard_rows, owns)
        ],
        in_specs=[SMEM] + [ANY] * (count + len(got)),
        out_specs=[pl.BlockSpec(memory_space=pltpu.VMEM)] * count,
        scratch_shapes=[pltpu.SemaphoreType.DMA((total,))],
        name="assemble",
    )(jnp.stack([where[0], where[1]]), *owns, *[g[2] for g in got])


def masked_scores(query_part, key_rows, segments, scaling):
    logits = jnp.einsum("qhd,khd->hqk", query_part, key_rows, preferred_element_type=F32) * scaling
    same_segment = segments[:, None] == segments[None, :]
    return jnp.where(same_segment[None], logits, -1e30)


def attend(queries, key_rows, value_rows, segments, scaling):
    logits = masked_scores(queries, key_rows, segments, scaling)
    row_max = jnp.max(logits, -1, keepdims=True)
    exponent = jnp.exp(logits - row_max)
    row_total = jnp.sum(exponent, -1, keepdims=True)
    softmax_low = (exponent / row_total).astype(BF)
    mixture = jnp.einsum("hqk,khd->qhd", softmax_low, value_rows, preferred_element_type=F32)
    return mixture.astype(BF), (row_max + jnp.log(row_total))[..., 0]


def attend_back(queries, key_rows, value_rows, segments, log_sums, grad_mixed, scaling):
    logits = masked_scores(queries, key_rows, segments, scaling)
    softmax_rows = jnp.exp(logits - log_sums[..., None])
    grad_soft = jnp.einsum("qhd,khd->hqk", grad_mixed, value_rows, preferred_element_type=F32)
    row_inner = jnp.sum(softmax_rows * grad_soft, -1, keepdims=True)
    grad_logits = (softmax_rows * (grad_soft - row_inner)).astype(BF)
    grad_queries = (
        jnp.einsum("hqk,khd->qhd", grad_logits, key_rows, preferred_element_type=F32) * scaling
    )
    grad_keys = (
        jnp.einsum("hqk,qhd->khd", grad_logits, queries, preferred_element_type=F32) * scaling
    )
    grad_values = jnp.einsum(
        "hqk,qhd->khd", softmax_rows.astype(BF), grad_mixed, preferred_element_type=F32
    )
    return grad_queries, grad_keys, grad_values


def shards(
    comm,
    tokens,
    cotangent,
    segment_ids,
    send_order,
    pack_order,
    query_weight,
    key_weight,
    value_weight,
    out_weight,
    up_weight,
    down_weight,
    *vectors,
):
    S = comm.S
    s = lax.axis_index("shard")
    c = lax.axis_index("rep") % 2
    pos = (s, c, S)
    row_count, width = tokens.shape
    send_rows = send_order[0]
    pack_rows = pack_order[0]
    segments = segment_ids[0]

    def exchange(rows):
        return lax.all_to_all(rows, ("rep", "shard"), split_axis=0, concat_axis=0, tiled=True)

    def my_half(weight):
        half = weight.shape[0] // 2
        return lax.dynamic_slice_in_dim(weight, c * half, half, 0)

    sizes = [v.shape[0] for v in vectors]
    packed = jnp.concatenate(vectors)
    packed = jnp.pad(packed, (0, VEC_ROWS * width - packed.shape[0])).reshape(VEC_ROWS, width)
    squares = (query_weight, key_weight, value_weight, out_weight)
    square_part = jnp.concatenate([my_half(w) for w in squares] + [packed])
    got_square = comm.gather(square_part)
    arrived = exchange(tokens[send_rows])
    got_up = comm.gather(my_half(up_weight))
    got_down = comm.gather(my_half(down_weight))
    arrived_grad = exchange(cotangent[send_rows])

    rows_shard = query_weight.shape[0]
    query_mat, key_mat, value_mat, out_mat, vec_all = assemble(
        pos,
        squares + (jnp.concatenate([packed, packed]),),
        got_square,
        [rows_shard] * 4 + [2 * VEC_ROWS],
        [rows_shard // 2] * 4 + [VEC_ROWS],
    )
    (up_mat,) = assemble(pos, (up_weight,), got_up, [rows_shard], [rows_shard // 2])
    down_rows = down_weight.shape[0]
    (down_mat,) = assemble(pos, (down_weight,), got_down, [down_rows], [down_rows // 2])
    vec_flat = vec_all.reshape(S, 2, VEC_ROWS * width)[:, 0]
    full_vectors = []
    at = 0
    for size in sizes:
        full_vectors.append(vec_flat[:, at : at + size].reshape(-1).astype(F32))
        at += size
    (
        query_add,
        value_add,
        out_add,
        up_add,
        down_add,
        gain_one,
        shift_one,
        gain_two,
        shift_two,
    ) = full_vectors

    inputs = arrived[pack_rows]
    grad_result = arrived_grad[pack_rows].astype(F32)
    scaling = HEAD_DIM ** (-0.5)
    head_shape = (row_count, HEADS, HEAD_DIM)
    queries = (project(inputs, query_mat) + query_add).astype(BF).reshape(head_shape)
    key_rows = project(inputs, key_mat).astype(BF).reshape(head_shape)
    value_rows = (project(inputs, value_mat) + value_add).astype(BF).reshape(head_shape)
    attended, log_sums = attend(queries, key_rows, value_rows, segments, scaling)
    attended = attended.reshape(row_count, -1)
    first_sum = inputs.astype(F32) + (project(attended, out_mat) + out_add)
    first_normed, first_spread = normalize(first_sum)
    normed_one = (first_normed * gain_one + shift_one).astype(BF)
    pre_act = project(normed_one, up_mat) + up_add
    activated = jax.nn.gelu(pre_act, approximate=False).astype(BF)
    second_sum = normed_one.astype(F32) + (project(activated, down_mat) + down_add)
    second_normed, second_spread = normalize(second_sum)
    layer_rows = (second_normed * gain_two + shift_two).astype(BF)
    inverse_pack = inverse(pack_rows)
    inverse_send = inverse(send_rows)
    layer_back = exchange(layer_rows[inverse_pack])[inverse_send]

    def split(grad):
        low = grad.astype(BF)
        rows = low.shape[0] // (2 * S)
        halves = low.reshape(S, 2, rows, low.shape[1])
        mine = lax.dynamic_index_in_dim(halves, c, 1, keepdims=False)
        theirs = lax.dynamic_index_in_dim(halves, 1 - c, 1, keepdims=False)
        return mine, theirs

    grad_gain_two = jnp.sum(grad_result * second_normed, 0)
    grad_shift_two = jnp.sum(grad_result, 0)
    grad_second = norm_back(grad_result * gain_two, second_normed, second_spread)
    grad_ffn = grad_second.astype(BF)
    grad_down = outer_sum(activated, grad_ffn)
    done_down = comm.reduce(*split(grad_down), s)
    grad_down_add = jnp.sum(grad_ffn.astype(F32), 0)
    gelu_slope = (
        0.5 * (1.0 + lax.erf(pre_act * inv_root_two))
        + pre_act * jnp.exp(-0.5 * pre_act * pre_act) * inv_root_tau
    )
    grad_pre = (project_back(grad_ffn, down_mat) * gelu_slope).astype(BF)
    grad_up = outer_sum(normed_one, grad_pre)
    done_up = comm.reduce(*split(grad_up), s)
    grad_up_add = jnp.sum(grad_pre.astype(F32), 0)
    grad_normed = grad_second + project_back(grad_pre, up_mat)
    grad_gain_one = jnp.sum(grad_normed * first_normed, 0)
    grad_shift_one = jnp.sum(grad_normed, 0)
    grad_first = norm_back(grad_normed * gain_one, first_normed, first_spread)
    grad_branch = grad_first.astype(BF)
    grad_out = outer_sum(attended, grad_branch)
    grad_out_add = jnp.sum(grad_branch.astype(F32), 0)
    grad_attended = project_back(grad_branch, out_mat).astype(BF).reshape(head_shape)
    grad_query_heads, grad_key_heads, grad_value_heads = attend_back(
        queries, key_rows, value_rows, segments, log_sums, grad_attended, scaling
    )
    grad_queries = grad_query_heads.reshape(row_count, -1).astype(BF)
    grad_keys = grad_key_heads.reshape(row_count, -1).astype(BF)
    grad_values = grad_value_heads.reshape(row_count, -1).astype(BF)
    grad_inputs = (
        grad_first
        + project_back(grad_queries, query_mat)
        + project_back(grad_keys, key_mat)
        + project_back(grad_values, value_mat)
    )
    grad_back = exchange(grad_inputs.astype(BF)[inverse_pack])[inverse_send]
    grad_query = outer_sum(inputs, grad_queries)
    grad_key = outer_sum(inputs, grad_keys)
    grad_value = outer_sum(inputs, grad_values)
    grad_query_add = jnp.sum(grad_queries.astype(F32), 0)
    grad_value_add = jnp.sum(grad_values.astype(F32), 0)
    small = [
        grad_query_add,
        grad_value_add,
        grad_out_add,
        grad_up_add,
        grad_down_add,
        grad_gain_one,
        grad_shift_one,
        grad_gain_two,
        grad_shift_two,
    ]
    small_rows = jnp.concatenate([v.reshape(S, -1) for v in small], 1)
    small_rows = jnp.pad(small_rows, ((0, 0), (0, VEC_ROWS * width - small_rows.shape[1])))
    small_rows = small_rows.reshape(S, VEC_ROWS, width).astype(BF)
    pairs = [split(g) for g in (grad_query, grad_key, grad_value, grad_out)]
    mine = jnp.concatenate([p[0] for p in pairs] + [small_rows], 1)
    theirs = jnp.concatenate([p[1] for p in pairs] + [small_rows], 1)
    done_square = comm.reduce(mine, theirs, s)

    def join(pair):
        low = jnp.where(c == 0, pair[0], pair[1])
        high = jnp.where(c == 0, pair[1], pair[0])
        return jnp.concatenate([low, high]).astype(F32)

    grads = []
    half = rows_shard // 2
    for w in range(4):
        grads.append(join([d[w * half : (w + 1) * half] for d in done_square]))
    grads.append(join(done_up))
    grads.append(join(done_down))
    flat = done_square[0][4 * half :].reshape(-1).astype(F32)
    at = 0
    for size in sizes:
        grads.append(flat[at : at + size])
        at += size
    return (layer_back, grad_back, *grads)


def solution(mesh):
    rows = P(("rep", "shard"), None)
    weight = P("shard", None)
    vector = P("shard")
    return jax.shard_map(
        functools.partial(shards, Comm(mesh)),
        mesh=mesh,
        in_specs=(rows,) * 5 + (weight,) * 6 + (vector,) * 9,
        out_specs=(rows,) * 2 + (weight,) * 6 + (vector,) * 9,
        check_vma=False,
    )
```
